128 devices in a mesh: walk: 4 (over x_lo, core), chol: 32 (over y, z, x_hi).
Axes of the slice: x: 4 (x_hi: 2, x_lo: 2; x = x_hi * 2 + x_lo), y: 4, z: 4, core: 2. Of those that a mesh axis runs over, the one named last changes fastest.
Arguments:
- walkers: bfloat16 [8, 32, 1024, 256], P('walk', 'chol'), may hold values from -1 to 2
- counts: int32 [8, 32], P('walk', 'chol'), may hold values from 0 to 3, as said below
- slot_copy: int32 [8, 32], P('walk', 'chol'), may hold values from 0 to 7, as said below
- factors: bfloat16 [32, 256, 1024], P('chol'), may hold values from -1 to 1
Outputs:
- combed: bfloat16 [8, 32, 1024, 256], P('walk', 'chol')
- gradient: float32 [8, 32, 1024, 256], P('walk', 'chol')
The draws below stay inside these ranges and needn't reach their ends.
Inputs may be any that keep to these rules, and one draw needn't show every extreme that they name: In each population (column) the counts sum to 8. `slot_copy`: each column is a permutation of the copy numbers 0 to 7.
All inputs are finite; a program needn't handle non-finite values.
Results may differ from the reference program's by a relative error of at most 0.0068.
Values may be sent and summed in bfloat16 or wider, within the bound.
No kernel may reach another device: no remote copies, remote signals or barrier semaphores. Data moves between devices by JAX's collectives and lax.ppermute only.
A program may use at most 64 MiB of HBM per device.

```python
import jax
import jax.numpy as jnp
from jax import lax

M = 1024
NEL = 256
CHOL_DEV = 1
NEWTON = 8
POP = 8
POPS = 32
CHOL = 32


def counts_column(column_key):
    shuffle = jax.random.permutation(column_key, POP)
    rank = jnp.zeros((POP,), jnp.int32).at[shuffle].set(jnp.arange(POP, dtype=jnp.int32))
    kinds = jax.random.randint(jax.random.fold_in(column_key, 7), (POP,), 0, 3)
    later = jnp.maximum(rank - 3, 0)
    pair_kind = kinds[later // 2]
    second = later % 2
    paired = jnp.where(pair_kind == 0, 1, jnp.where(pair_kind == 1, 2 - 2 * second, 2 * second))
    single = ((POP - 3) % 2 == 1) & (rank == POP - 1)
    return jnp.where(rank == 0, 3, jnp.where(rank < 3, 0, jnp.where(single, 1, paired))).astype(jnp.int32)


def draw_counts(key, part):

    def fold_column(column_index):
        return jax.random.fold_in(key, column_index)
    column_keys = jax.vmap(fold_column)(jnp.arange(POPS))
    columns = jax.vmap(counts_column)(column_keys)
    return columns.T


def draw_slot_copy(key, part):

    def permute_column(column_index):
        column_key = jax.random.fold_in(key, 100000 + column_index)
        return jax.random.permutation(column_key, POP).astype(jnp.int32)
    columns = jax.vmap(permute_column)(jnp.arange(POPS))
    return columns.T


def draw_walkers(key, part):
    key_top = jax.random.fold_in(key, 11)
    key_low = jax.random.fold_in(key, 12)
    noise_top = jnp.clip(jax.random.normal(key_top, (POP, POPS, NEL, NEL), jnp.float32), -4.0, 4.0)
    noise_low = jnp.clip(jax.random.normal(key_low, (POP, POPS, M - NEL, NEL), jnp.float32), -4.0, 4.0)
    spread = 1.0 / NEL ** 0.5
    skewed = 0.75 * spread * (noise_top - jnp.swapaxes(noise_top, -1, -2)) / 1.4142136
    identity = jnp.broadcast_to(jnp.eye(NEL, dtype=jnp.float32), skewed.shape)
    rotation = jnp.linalg.solve(identity - skewed, identity + skewed)
    upper = identity + 0.985 * rotation
    lower = spread * noise_low
    return jnp.concatenate([upper, lower], axis=2).astype(jnp.bfloat16)


def shard_levels(key, shape, split, least, largest):
    factor_of, own = 1.0, jax.random.fold_in(key, 6)
    for position, shards_of in split:
        draws = jnp.exp(jax.random.uniform(jax.random.fold_in(own, position), (shards_of,), jnp.float32, least / len(split), largest / len(split)))
        factor_of = factor_of * jnp.repeat(draws, shape[position] // shards_of).reshape([-1 if axis == position else 1 for axis in range(len(shape))])
    return factor_of


def noise(rng, dims, scale, bound, cuts=(), kind=jnp.bfloat16):
    loudness = shard_levels(rng, dims, cuts, -0.22, 0.18) if cuts else 1.0
    entries = jax.random.normal(rng, dims, jnp.float32) * scale * loudness
    return jnp.minimum(jnp.maximum(entries, -bound), bound).astype(kind)


def setup_inputs(seed: int = 0) -> dict:
    key_list = jax.random.split(jax.random.key(seed), 5)
    walkers = draw_walkers(jax.random.fold_in(key_list[4], 71), 0)
    counts = draw_counts(jax.random.fold_in(key_list[4], 71), 0)
    slot_copy = draw_slot_copy(jax.random.fold_in(key_list[4], 71), 0)
    factors = noise(key_list[3], (CHOL, NEL, M), ((4 * CHOL * NEL) ** -0.25), 1.0, ((0, 32),))
    return dict(walkers=walkers, counts=counts, slot_copy=slot_copy, factors=factors)


def reference(walkers, counts, slot_copy, factors):
    inclusive = jnp.cumsum(counts, axis=0).astype(jnp.int32)
    copy_index = jnp.arange(POP, dtype=jnp.int32)
    parent = jnp.sum((inclusive[None, :, :] <= copy_index[:, None, None]).astype(jnp.int32), axis=1).astype(jnp.int32)
    source = jnp.take_along_axis(parent, slot_copy, axis=0)
    column = jnp.arange(POPS, dtype=jnp.int32)[None, :]
    combed = walkers[source, column]
    intersection = combed[:, :, :NEL, :].astype(jnp.float32)
    identity = jnp.eye(NEL, dtype=jnp.float32)
    inverse = jnp.broadcast_to(identity, intersection.shape)
    for newton_step in range(NEWTON):
        product = jnp.einsum('pcij,pcjk->pcik', intersection, inverse, precision=lax.Precision.HIGHEST)
        inverse = jnp.einsum('pcij,pcjk->pcik', inverse, 2.0 * identity - product, precision=lax.Precision.HIGHEST)
    inverse_half = inverse.astype(jnp.bfloat16)
    green = jnp.einsum('pcmj,pcji->pcmi', combed.astype(jnp.float32), inverse_half.astype(jnp.float32)).astype(jnp.bfloat16)
    green_full = green.astype(jnp.float32)
    blocks = factors.reshape(POPS, CHOL_DEV, NEL, M)

    def accumulate(running, factor_block):
        block_full = factor_block.astype(jnp.float32)
        rotated = jnp.einsum('lrm,pcmq->pclrq', block_full, green_full).astype(jnp.bfloat16)
        rotated_full = lax.optimization_barrier(rotated).astype(jnp.float32)
        shard_grad = -jnp.einsum('lam,pclia->pcmi', block_full, rotated_full)
        shard_grad = lax.optimization_barrier(shard_grad.astype(jnp.bfloat16)).astype(jnp.float32)
        return (running + shard_grad, None)
    gradient, unused = lax.scan(accumulate, jnp.zeros(green.shape, jnp.float32), blocks)
    return (combed, gradient)
```

```python
import functools

import jax
import jax.numpy as jnp
from jax import lax
from jax.experimental import pallas as pl
from jax.experimental.pallas import tpu as pltpu
from jax.sharding import PartitionSpec as P

NEL = 256
M = 1024
NEWTON = 8
MIB = 1 << 20


BF16 = jnp.bfloat16
F32 = jnp.float32
VM = pl.BlockSpec(memory_space=pltpu.VMEM)
SM = pl.BlockSpec(memory_space=pltpu.SMEM)


def dot(a, b):
    return jnp.dot(a, b, preferred_element_type=F32)


def line(x_lo, core, y, z, x_hi):
    return (x_lo * 2 + core) * 32 + (y * 4 + z) * 2 + x_hi


def moved(x, where):
    pairs = []
    for x_lo in range(2):
        for core in range(2):
            for y in range(4):
                for z in range(4):
                    for x_hi in range(2):
                        here = (x_lo, core, y, z, x_hi)
                        pairs.append((line(*here), line(*where(*here))))
    return lax.ppermute(x, ("walk", "chol"), pairs)


def to_core(x):
    return moved(x, lambda xl, c, y, z, xh: (xl, 1 - c, y, z, xh))


def to_pair(x):
    return moved(x, lambda xl, c, y, z, xh: (1 - xl, c, y, z, xh))


def swap_factor(x):
    def where(xl, c, y, z, xh):
        return (xl, c, y, z, xh) if c == xh else (1 - xl, 1 - c, y, z, 1 - xh)

    return moved(x, where)


def along_a(x, s):
    def where(xl, c, y, z, xh):
        return (xl, c, (y + s) % 4, z, xh) if c == 0 else (xl, c, y, (z + s) % 4, xh)

    return moved(x, where)


def along_b(x, s):
    def where(xl, c, y, z, xh):
        return (xl, c, y, (z + s) % 4, xh) if c == 0 else (xl, c, (y + s) % 4, z, xh)

    return moved(x, where)


def source_kernel(my_ref, count_ref, slot_ref, out_ref):
    my = my_ref[0]
    running = jnp.int32(0)
    inclusive = []
    for d in range(4):
        for i in range(2):
            running = running + count_ref[(my ^ d) * 2 + i]
            inclusive.append(running)
    for s in range(4):
        n = jnp.int32(0)
        for value in inclusive:
            n = n + jnp.where(value <= slot_ref[s], 1, 0)
        n = jnp.minimum(n, 7)
        out_ref[s] = (((n >> 1) ^ my) << 1) + (n & 1)


def find_sources(my, counts, slots):
    return pl.pallas_call(
        source_kernel,
        in_specs=[SM, SM, SM],
        out_specs=SM,
        out_shape=jax.ShapeDtypeStruct((4,), jnp.int32),
        name="sources",
    )(my, counts, slots)


def pick(source, refs, store):
    for j, ref in enumerate(refs):

        @pl.when((source >> 1) == j)
        def _():
            i = source & 1
            store(ref[i, 0] if len(ref.shape) == 4 else ref[i])


def newton_kernel(src_ref, own_ref, core_ref, pair_ref, diag_ref, out_ref, a_ref, x_ref):
    row = lax.broadcasted_iota(jnp.int32, (NEL, NEL), 0)
    col = lax.broadcasted_iota(jnp.int32, (NEL, NEL), 1)
    twice = jnp.where(row == col, 2.0, 0.0).astype(F32)
    refs = (own_ref, core_ref, pair_ref, diag_ref)
    for s in range(2):

        def store(value, s=s):
            a_ref[s] = value

        pick(src_ref[s], refs, store)
    for s in range(2):
        x_ref[s] = twice - a_ref[s].astype(F32)

    def step(k, carry):
        for s in range(2):
            x = x_ref[s]
            hi = x.astype(BF16)
            lo = (x - hi.astype(F32)).astype(BF16)
            a = a_ref[s]
            t = twice - (dot(a, hi) + dot(a, lo))
            t_hi = t.astype(BF16)
            t_lo = (t - t_hi.astype(F32)).astype(BF16)
            x_ref[s] = dot(hi, t_hi) + (dot(hi, t_lo) + dot(lo, t_hi))
        return carry

    lax.fori_loop(0, NEWTON - 1, step, 0)
    for s in range(2):
        out_ref[s] = x_ref[s].astype(BF16)


def newton(src, own, core, pair0, diag0):
    top = pl.BlockSpec((2, 1, NEL, NEL), lambda i: (0, 0, 0, 0))
    return pl.pallas_call(
        newton_kernel,
        grid=(1,),
        in_specs=[SM, top, top, VM, VM],
        out_specs=VM,
        out_shape=jax.ShapeDtypeStruct((2, NEL, NEL), BF16),
        scratch_shapes=[pltpu.VMEM((2, NEL, NEL), BF16), pltpu.VMEM((2, NEL, NEL), F32)],
        compiler_params=pltpu.CompilerParams(vmem_limit_bytes=12 * MIB),
        name="newton",
    )(src, own, core, pair0, diag0)


def green_kernel(src_ref, own_ref, core_ref, pair_ref, diag_ref, inv_ref, inv_p_ref, *rest, at, rows):
    combed_ref, green_ref, c_ref = rest[-3:]
    refs = (own_ref, core_ref, pair_ref, diag_ref)
    for s in range(4):

        def store(value, s=s):
            c_ref[s] = value

        pick(src_ref[s], refs, store)
    for s in range(4):
        inv = inv_ref[s] if s < 2 else inv_p_ref[s - 2]
        green_ref[s, at : at + rows] = dot(c_ref[s], inv).astype(BF16)
        if s < 2:
            combed_ref[s, 0] = c_ref[s]


def green_piece(src, own, core, pair, diag, inv, inv_p, so_far, at):
    rows = pair.shape[1]
    block = pl.BlockSpec((2, 1, rows, NEL), lambda i: (0, 0, at // rows, 0))
    carried = [] if so_far is None else list(so_far)
    return pl.pallas_call(
        functools.partial(green_kernel, at=at, rows=rows),
        grid=(1,),
        in_specs=[SM, block, block, VM, VM, VM, VM]
        + ([pl.BlockSpec(memory_space=pl.ANY), VM] if carried else []),
        out_specs=[block, VM],
        out_shape=[
            jax.ShapeDtypeStruct((2, 1, M, NEL), BF16),
            pltpu.VMEM((4, M, NEL), BF16),
        ],
        scratch_shapes=[pltpu.VMEM((4, rows, NEL), BF16)],
        input_output_aliases={7: 0, 8: 1} if carried else {},
        compiler_params=pltpu.CompilerParams(vmem_limit_bytes=16 * MIB),
        name=f"green{at}",
    )(src, own, core, pair, diag, inv, inv_p, *carried)


def pair_products(f_refs, green_ref, walkers, rot_ref):
    for l, f in enumerate(f_refs):
        for i, w in enumerate(walkers):
            rot_ref[i * NEL : (i + 1) * NEL, l * NEL : (l + 1) * NEL] = dot(
                f[...], green_ref[w]
            ).astype(BF16)


def main_kernel(*refs, n, first):
    f_refs, green_ref = refs[:n], refs[n]
    out_ref, rot_ref = refs[-2:]
    pair_products(f_refs, green_ref, range(4), rot_ref)
    stacked = jnp.concatenate([f[...] for f in f_refs], axis=0)
    for m in range(0, M, NEL):
        added = dot(rot_ref[...], stacked[:, m : m + NEL])
        out_ref[:, m : m + NEL] = added if first else refs[n + 1][:, m : m + NEL] + added


def main_part(blocks, green, running):
    n = len(blocks)
    first = running is None
    operands = list(blocks) + [green] + ([] if first else [running])
    return pl.pallas_call(
        functools.partial(main_kernel, n=n, first=first),
        in_specs=[VM] * len(operands),
        out_specs=VM,
        out_shape=pltpu.VMEM((4 * NEL, M), F32),
        scratch_shapes=[pltpu.VMEM((4 * NEL, n * NEL), BF16)],
        input_output_aliases={} if first else {n + 1: 0},
        compiler_params=pltpu.CompilerParams(vmem_limit_bytes=24 * MIB),
        cost_estimate=pl.CostEstimate(
            flops=n * 16 * NEL * NEL * M, transcendentals=0, bytes_accessed=n * MIB // 2
        ),
        name=f"main{n}",
    )(*operands)


def last_kernel(*refs, n, low):
    f_refs, green_ref, acc_ref, out_ref, rot_ref = refs[:n], refs[n], refs[n + 1], refs[-2], refs[-1]
    pair_products(f_refs, green_ref, (low, low + 1), rot_ref)
    stacked = jnp.concatenate([f[...] for f in f_refs], axis=0)
    for m in range(0, M, NEL):
        added = dot(rot_ref[...], stacked[:, m : m + NEL])
        total = acc_ref[low * NEL : (low + 2) * NEL, m : m + NEL] + added
        out_ref[:, m : m + NEL] = total.astype(out_ref.dtype)


def last_part(blocks, green, running, low, out_shape):
    n = len(blocks)
    return pl.pallas_call(
        functools.partial(last_kernel, n=n, low=low),
        in_specs=[VM] * (n + 2),
        out_specs=VM,
        out_shape=out_shape,
        scratch_shapes=[pltpu.VMEM((2 * NEL, n * NEL), BF16)],
        compiler_params=pltpu.CompilerParams(vmem_limit_bytes=24 * MIB),
        cost_estimate=pl.CostEstimate(
            flops=n * 8 * NEL * NEL * M, transcendentals=0, bytes_accessed=n * MIB // 2
        ),
        name=f"last{low}",
    )(*blocks, green, running)


def combine_kernel(own_ref, other_ref, out_ref):
    out_ref[0, 0] = -(own_ref[...] + other_ref[...].astype(F32)).T


def combine(own, other):
    part = pl.BlockSpec((NEL, M), lambda w: (w, 0))
    return pl.pallas_call(
        combine_kernel,
        grid=(2,),
        in_specs=[part, part],
        out_specs=pl.BlockSpec((1, 1, M, NEL), lambda w: (w, 0, 0, 0)),
        out_shape=jax.ShapeDtypeStruct((2, 1, M, NEL), F32),
        compiler_params=pltpu.CompilerParams(vmem_limit_bytes=16 * MIB),
        name="combine",
    )(own, other)


def body(walkers, counts, slot_copy, factors):
    swapped = swap_factor(factors.reshape(NEL, M))
    core_w = to_core(walkers)
    pair0 = to_pair(walkers[:, 0, :NEL])
    small = jnp.concatenate([counts[:, 0], slot_copy[:, 0]])
    small_c = to_core(small)
    near = jnp.concatenate([counts[:, 0], small_c[:2]])
    far = to_pair(near)
    slots = jnp.concatenate([slot_copy[:, 0], small_c[2:]])
    pair1 = to_pair(walkers[:, 0, 2 * NEL :])
    pair2 = to_pair(walkers[:, 0, NEL : 2 * NEL])
    my = lax.axis_index("walk").astype(jnp.int32).reshape(1)
    src = find_sources(my, jnp.concatenate([near, far]), slots)
    diag0 = to_core(pair0)
    inv = newton(src, walkers, core_w, pair0, diag0)
    inv_p = to_core(inv)

    have = {(0, 0): swapped}
    have[-1, 0] = along_a(have[0, 0], 1)
    have[1, 0] = along_a(have[0, 0], -1)
    have[0, -1] = along_b(have[0, 0], 1)
    have[0, 1] = along_b(have[0, 0], -1)
    have[2, 0] = along_a(have[-1, 0], 1)
    have[-1, -1] = along_b(have[-1, 0], 1)
    have[-1, 1] = along_b(have[-1, 0], -1)
    have[1, -1] = along_b(have[1, 0], 1)
    have[1, 1] = along_b(have[1, 0], -1)
    have[2, -1] = along_b(have[2, 0], 1)
    have[2, 1] = along_b(have[2, 0], -1)
    have[0, 2] = along_b(have[0, -1], 1)
    have[-1, 2] = along_b(have[-1, 1], -1)
    have[1, 2] = along_b(have[1, -1], 1)
    have[2, 2] = along_b(have[2, 1], -1)

    green = green_piece(src, walkers, core_w, pair0, diag0, inv, inv_p, None, 0)
    diag1 = to_core(pair1)
    green = green_piece(src, walkers, core_w, pair1, diag1, inv, inv_p, green, 2 * NEL)
    diag2 = to_core(pair2)
    combed, green = green_piece(src, walkers, core_w, pair2, diag2, inv, inv_p, green, NEL)

    running = None
    for group in (
        ((0, 0), (-1, 0), (1, 0), (0, -1), (0, 1)),
        ((2, 0), (-1, -1), (-1, 1)),
        ((1, -1), (1, 1)),
        ((2, -1), (2, 1)),
        ((0, 2), (-1, 2)),
    ):
        running = main_part([have[at] for at in group], green, running)
    blocks = [have[1, 2], have[2, 2]]
    other = to_core(
        last_part(blocks, green, running, 2, jax.ShapeDtypeStruct((2 * NEL, M), BF16))
    )
    own = last_part(blocks, green, running, 0, pltpu.VMEM((2 * NEL, M), F32))
    return combed, combine(own, other)


def solution(mesh):
    in_specs = (
        P("walk", "chol", None, None),
        P("walk", "chol"),
        P("walk", "chol"),
        P("chol", None, None),
    )
    out_specs = (P("walk", "chol", None, None), P("walk", "chol", None, None))
    return jax.shard_map(body, mesh=mesh, in_specs=in_specs, out_specs=out_specs, check_vma=False)
```

```python
import functools

import jax
import jax.numpy as jnp
from jax import lax
from jax.experimental import pallas as pl
from jax.experimental.pallas import tpu as pltpu
from jax.sharding import PartitionSpec as P

NEL = 256
M = 1024
NEWTON = 8
MIB = 1 << 20


BF16 = jnp.bfloat16
F32 = jnp.float32
VM = pl.BlockSpec(memory_space=pltpu.VMEM)
SM = pl.BlockSpec(memory_space=pltpu.SMEM)


def dot(a, b):
    return jnp.dot(a, b, preferred_element_type=F32)


def line(x_lo, core, y, z, x_hi):
    return (x_lo * 2 + core) * 32 + (y * 4 + z) * 2 + x_hi


def moved(x, where):
    pairs = []
    for x_lo in range(2):
        for core in range(2):
            for y in range(4):
                for z in range(4):
                    for x_hi in range(2):
                        here = (x_lo, core, y, z, x_hi)
                        pairs.append((line(*here), line(*where(*here))))
    return lax.ppermute(x, ("walk", "chol"), pairs)


def to_core(x):
    return moved(x, lambda xl, c, y, z, xh: (xl, 1 - c, y, z, xh))


def to_pair(x):
    return moved(x, lambda xl, c, y, z, xh: (1 - xl, c, y, z, xh))


def swap_factor(x):
    def where(xl, c, y, z, xh):
        return (xl, c, y, z, xh) if c == xh else (1 - xl, 1 - c, y, z, 1 - xh)

    return moved(x, where)


def along_a(x, s):
    def where(xl, c, y, z, xh):
        return (xl, c, (y + s) % 4, z, xh) if c == 0 else (xl, c, y, (z + s) % 4, xh)

    return moved(x, where)


def along_b(x, s):
    def where(xl, c, y, z, xh):
        return (xl, c, y, (z + s) % 4, xh) if c == 0 else (xl, c, (y + s) % 4, z, xh)

    return moved(x, where)


def pick(source, refs, store):
    for j, ref in enumerate(refs):

        @pl.when((source >> 1) == j)
        def _():
            store(ref, source & 1)


def find_sources(my, refs, src_ref):
    info = [[ref[i, NEL : NEL + 16, 0:128].astype(F32) for i in range(2)] for ref in refs]
    count = {(r, i): info[r][i][0:1] for r in range(4) for i in range(2)}
    position = {(r, i): (my ^ r) * 2 + i for r in range(4) for i in range(2)}
    upto = {}
    for here in count:
        total = count[here]
        for there in count:
            if there != here:
                total = total + jnp.where(position[there] < position[here], count[there], 0.0)
        upto[here] = total
    found = []
    for s in range(4):
        slot = info[s // 2][s % 2][1:2]
        chosen = jnp.zeros_like(slot)
        for r, i in count:
            inside = (upto[r, i] > slot) & (upto[r, i] - count[r, i] <= slot)
            chosen = chosen + jnp.where(inside, float(2 * r + i), 0.0)
        found.append(jnp.max(chosen).astype(jnp.int32))
        src_ref[s] = found[s]
    return found


def newton_kernel(my_ref, own_ref, core_ref, pair_ref, diag_ref, src_ref, inv_ref, a_ref, x_ref, r_ref, z_ref):
    refs = (own_ref, core_ref, pair_ref, diag_ref)
    found = find_sources(my_ref[0], refs, src_ref)
    row = lax.broadcasted_iota(jnp.int32, (NEL, NEL), 0)
    col = lax.broadcasted_iota(jnp.int32, (NEL, NEL), 1)
    one = jnp.where(row == col, 1.0, 0.0).astype(F32)
    for s in range(4):

        def store(ref, i, s=s):
            a_ref[s] = ref[i, 0:NEL]

        pick(found[s], refs, store)

    def split(value, high, low):
        upper = value.astype(BF16)
        z_ref[high] = upper
        z_ref[low] = (value - upper.astype(F32)).astype(BF16)

    def blocks(s):
        at = s * 4
        return at, at + 1, at + 2, at + 3

    for s in range(4):
        xh, rh, xl, rl = blocks(s)
        residual = one - a_ref[s].astype(F32)
        split(residual, rh, rl)
        x_ref[s] = one + residual
    for s in range(4):
        xh, rh, xl, rl = blocks(s)
        r_ref[s] = dot(z_ref[rh], z_ref[rh]) + (dot(z_ref[rh], z_ref[rl]) + dot(z_ref[rl], z_ref[rh]))

    def step(k, carry):
        for s in range(4):
            xh, rh, xl, rl = blocks(s)
            split(x_ref[s], xh, xl)
            split(r_ref[s], rh, rl)
        for s in range(4):
            xh, rh, xl, rl = blocks(s)
            both = z_ref[xh : xh + 4].reshape(4 * NEL, NEL)
            by_high = dot(both, z_ref[rh])
            by_low = dot(both[: 2 * NEL], z_ref[rl])
            x_ref[s] = x_ref[s] + (by_high[:NEL] + (by_high[2 * NEL : 3 * NEL] + by_low[:NEL]))
            r_ref[s] = by_high[NEL : 2 * NEL] + (by_high[3 * NEL :] + by_low[NEL:])
        return carry

    lax.fori_loop(0, NEWTON - 2, step, 0)
    for s in range(4):
        xh, rh, xl, rl = blocks(s)
        split(x_ref[s], xh, xl)
        split(r_ref[s], rh, rl)
    for s in range(4):
        xh, rh, xl, rl = blocks(s)
        last = dot(z_ref[xh], z_ref[rh]) + (dot(z_ref[xh], z_ref[rl]) + dot(z_ref[xl], z_ref[rh]))
        inv_ref[s] = (x_ref[s] + last).astype(BF16)


def newton(my, own, core, pair, diag):
    return pl.pallas_call(
        newton_kernel,
        in_specs=[SM, VM, VM, VM, VM],
        out_specs=[SM, VM],
        out_shape=[
            jax.ShapeDtypeStruct((4,), jnp.int32),
            pltpu.VMEM((4, NEL, NEL), BF16),
        ],
        scratch_shapes=[
            pltpu.VMEM((4, NEL, NEL), BF16),
            pltpu.VMEM((4, NEL, NEL), F32),
            pltpu.VMEM((4, NEL, NEL), F32),
            pltpu.VMEM((16, NEL, NEL), BF16),
        ],
        compiler_params=pltpu.CompilerParams(vmem_limit_bytes=16 * MIB),
        name="newton",
    )(my, own, core, pair, diag)


def green_kernel(src_ref, own_ref, core_ref, pair_ref, diag_ref, inv_ref, *rest, at, rows):
    green_ref, new_ref, c_ref = rest[-3:]
    refs = (own_ref, core_ref, pair_ref, diag_ref)
    for s in range(4):

        def store(ref, i, s=s):
            if s < 2:
                new_ref[s, at : at + rows] = ref[i, 0:rows]
            else:
                c_ref[s - 2] = ref[i, 0:rows]

        pick(src_ref[s], refs, store)
    for s in range(4):
        c = new_ref[s, at : at + rows] if s < 2 else c_ref[s - 2]
        green_ref[s, at : at + rows] = dot(c, inv_ref[s]).astype(BF16)


def green_piece(src, own, core, pair, diag, inv, so_far, at, rows):
    carried = [] if so_far is None else list(so_far)
    return pl.pallas_call(
        functools.partial(green_kernel, at=at, rows=rows),
        in_specs=[SM] + [VM] * (5 + len(carried)),
        out_specs=[VM, VM],
        out_shape=[pltpu.VMEM((4, M, NEL), BF16), pltpu.VMEM((2, M, NEL), BF16)],
        scratch_shapes=[pltpu.VMEM((2, rows, NEL), BF16)],
        input_output_aliases={6: 0, 7: 1} if carried else {},
        compiler_params=pltpu.CompilerParams(vmem_limit_bytes=16 * MIB),
    )(src, own, core, pair, diag, inv, *carried)


def load_blocks(refs):
    found = []
    for ref in refs:
        found += [ref[...]] if len(ref.shape) == 2 else [ref[i] for i in range(ref.shape[0])]
    return found


def count_blocks(arrays):
    return sum(1 if a.ndim == 2 else a.shape[0] for a in arrays)


def pair_products(blocks, green_ref, walkers, rot_ref):
    for l, f in enumerate(blocks):
        for i, w in enumerate(walkers):
            rot_ref[i * NEL : (i + 1) * NEL, l * NEL : (l + 1) * NEL] = dot(f, green_ref[w]).astype(BF16)
    return jnp.concatenate(blocks, axis=0)


def first_kernel(*refs, n):
    f_refs, green_ref, new_ref = refs[:n], refs[n], refs[n + 1]
    out_ref, combed_ref, rot_ref, sem = refs[n + 2 :]
    copy = pltpu.make_async_copy(new_ref, combed_ref.at[:, 0], sem)
    copy.start()
    stacked = pair_products(load_blocks(f_refs), green_ref, range(4), rot_ref)
    for m in range(0, M, NEL):
        out_ref[:, m : m + NEL] = dot(rot_ref[...], stacked[:, m : m + NEL])
    copy.wait()


def first_part(arrays, green, new):
    n, count = len(arrays), count_blocks(arrays)
    return pl.pallas_call(
        functools.partial(first_kernel, n=n),
        in_specs=[VM] * (n + 2),
        out_specs=[VM, pl.BlockSpec(memory_space=pl.ANY)],
        out_shape=[pltpu.VMEM((4 * NEL, M), F32), jax.ShapeDtypeStruct((2, 1, M, NEL), BF16)],
        scratch_shapes=[pltpu.VMEM((4 * NEL, count * NEL), BF16), pltpu.SemaphoreType.DMA],
        compiler_params=pltpu.CompilerParams(vmem_limit_bytes=24 * MIB),
        cost_estimate=pl.CostEstimate(
            flops=count * 16 * NEL * NEL * M, transcendentals=0, bytes_accessed=count * MIB // 2
        ),
    )(*arrays, green, new)


def main_kernel(*refs, n):
    f_refs, green_ref, acc_ref, out_ref, rot_ref = refs[:n], refs[n], refs[n + 1], refs[-2], refs[-1]
    stacked = pair_products(load_blocks(f_refs), green_ref, range(4), rot_ref)
    for m in range(0, M, NEL):
        out_ref[:, m : m + NEL] = acc_ref[:, m : m + NEL] + dot(rot_ref[...], stacked[:, m : m + NEL])


def main_part(arrays, green, running):
    n, count = len(arrays), count_blocks(arrays)
    return pl.pallas_call(
        functools.partial(main_kernel, n=n),
        in_specs=[VM] * (n + 2),
        out_specs=VM,
        out_shape=pltpu.VMEM((4 * NEL, M), F32),
        scratch_shapes=[pltpu.VMEM((4 * NEL, count * NEL), BF16)],
        input_output_aliases={n + 1: 0},
        compiler_params=pltpu.CompilerParams(vmem_limit_bytes=24 * MIB),
        cost_estimate=pl.CostEstimate(
            flops=count * 16 * NEL * NEL * M, transcendentals=0, bytes_accessed=count * MIB // 2
        ),
    )(*arrays, green, running)


def last_kernel(*refs, n, low):
    f_refs, green_ref, acc_ref, out_ref, rot_ref = refs[:n], refs[n], refs[n + 1], refs[-2], refs[-1]
    stacked = pair_products(load_blocks(f_refs), green_ref, (low, low + 1), rot_ref)
    for m in range(0, M, NEL):
        added = dot(rot_ref[...], stacked[:, m : m + NEL])
        total = acc_ref[low * NEL : (low + 2) * NEL, m : m + NEL] + added
        out_ref[:, m : m + NEL] = total.astype(out_ref.dtype)


def last_part(arrays, green, running, low, out_shape):
    n, count = len(arrays), count_blocks(arrays)
    return pl.pallas_call(
        functools.partial(last_kernel, n=n, low=low),
        in_specs=[VM] * (n + 2),
        out_specs=VM,
        out_shape=out_shape,
        scratch_shapes=[pltpu.VMEM((2 * NEL, count * NEL), BF16)],
        compiler_params=pltpu.CompilerParams(vmem_limit_bytes=24 * MIB),
        cost_estimate=pl.CostEstimate(
            flops=count * 8 * NEL * NEL * M, transcendentals=0, bytes_accessed=count * MIB // 2
        ),
    )(*arrays, green, running)


def combine_kernel(own_ref, other_ref, out_ref):
    out_ref[0, 0] = -(own_ref[...] + other_ref[...].astype(F32)).T


def combine(own, other):
    part = pl.BlockSpec((NEL, M), lambda w: (w, 0))
    return pl.pallas_call(
        combine_kernel,
        grid=(2,),
        in_specs=[part, part],
        out_specs=pl.BlockSpec((1, 1, M, NEL), lambda w: (w, 0, 0, 0)),
        out_shape=jax.ShapeDtypeStruct((2, 1, M, NEL), F32),
        compiler_params=pltpu.CompilerParams(vmem_limit_bytes=16 * MIB),
        name="combine",
    )(own, other)


def step(walkers, counts, slot_copy, factors):
    swapped = swap_factor(factors.reshape(NEL, M))
    kind = lax.broadcasted_iota(jnp.int32, (2, 16, NEL), 1)
    info = jnp.where(kind == 0, counts[:, :, None], slot_copy[:, :, None]).astype(BF16)
    top = jnp.concatenate([walkers[:, 0, :NEL], info], axis=1)
    pair_top = to_pair(top)
    core_top = to_core(top)
    rest = walkers[:, 0, NEL:]
    pair_rest = to_pair(rest)
    core_rest = to_core(rest)
    diag_top = to_core(pair_top)
    my = lax.axis_index("walk").astype(jnp.int32).reshape(1)
    src, inv = newton(my, top, core_top, pair_top, diag_top)

    f = {(0, 0): swapped}
    f[-1, 0] = along_a(swapped, 1)
    f[1, 0] = along_a(swapped, -1)
    f[0, -1] = along_b(swapped, 1)
    f[0, 1] = along_b(swapped, -1)
    f[2, 0] = along_a(f[-1, 0], 1)
    sides = jnp.stack([f[-1, 0], f[1, 0]])
    sides_below = along_b(sides, 1)
    sides_above = along_b(sides, -1)
    f[0, 2] = along_b(f[0, 1], -1)
    f[2, -1] = along_b(f[2, 0], 1)
    f[2, 1] = along_b(f[2, 0], -1)
    sides_far = along_b(sides_below, 1)
    f[2, 2] = along_b(f[2, 1], -1)

    part = green_piece(src, top, core_top, pair_top, diag_top, inv, None, 0, NEL)
    diag_rest = to_core(pair_rest)
    green, new = green_piece(src, rest, core_rest, pair_rest, diag_rest, inv, part, NEL, M - NEL)

    running, combed = first_part([f[0, 0], f[-1, 0], f[1, 0], f[0, -1], f[0, 1]], green, new)
    running = main_part([f[2, 0], f[0, 2]], green, running)
    running = main_part([sides_below, sides_above], green, running)
    running = main_part([f[2, -1], f[2, 1]], green, running)
    blocks = [sides_far, f[2, 2]]
    half = (2 * NEL, M)
    other = to_core(last_part(blocks, green, running, 2, jax.ShapeDtypeStruct(half, BF16)))
    own = last_part(blocks, green, running, 0, pltpu.VMEM(half, F32))
    return combed, combine(own, other)


def solution(mesh):
    in_specs = (
        P("walk", "chol", None, None),
        P("walk", "chol"),
        P("walk", "chol"),
        P("chol", None, None),
    )
    out_specs = (P("walk", "chol", None, None), P("walk", "chol", None, None))
    return jax.shard_map(step, mesh=mesh, in_specs=in_specs, out_specs=out_specs, check_vma=False)
```

```python
import functools

import jax
import jax.numpy as jnp
from jax import lax
from jax.experimental import pallas as pl
from jax.experimental.pallas import tpu as pltpu
from jax.sharding import PartitionSpec as P

NEL = 256
M = 1024
NEWTON = 8
MIB = 1 << 20


BF16 = jnp.bfloat16
F32 = jnp.float32
VM = pl.BlockSpec(memory_space=pltpu.VMEM)
SM = pl.BlockSpec(memory_space=pltpu.SMEM)
HBM = pl.BlockSpec(memory_space=pltpu.HBM)


def dot(a, b):
    return jnp.dot(a, b, preferred_element_type=F32)


def line(x_lo, core, y, z, x_hi):
    return (x_lo * 2 + core) * 32 + (y * 4 + z) * 2 + x_hi


def moved(x, where):
    pairs = []
    for x_lo in range(2):
        for core in range(2):
            for y in range(4):
                for z in range(4):
                    for x_hi in range(2):
                        here = (x_lo, core, y, z, x_hi)
                        there = where(*here)
                        if there is not None:
                            pairs.append((line(*here), line(*there)))
    return lax.ppermute(x, ("walk", "chol"), pairs)


def to_core(x):
    return moved(x, lambda xl, c, y, z, xh: (xl, 1 - c, y, z, xh))


def to_pair(x):
    return moved(x, lambda xl, c, y, z, xh: (1 - xl, c, y, z, xh))


def swap_factor(x):
    def where(xl, c, y, z, xh):
        return None if c == xh else (1 - xl, 1 - c, y, z, 1 - xh)

    return moved(x, where)


def shifted(core, y, z, along, s):
    on_y = (core == 0) == (along == "a")
    return ((y + s) % 4, z) if on_y else (y, (z + s) % 4)


def first_along(x, along, s):
    def where(xl, c, y, z, xh):
        if c == xh:
            return (xl, c, *shifted(c, y, z, along, s), xh)
        return (1 - xl, 1 - c, *shifted(1 - c, y, z, along, s), 1 - xh)

    return moved(x, where)


def along_b(x, s):
    return moved(x, lambda xl, c, y, z, xh: (xl, c, *shifted(c, y, z, "b", s), xh))


def held(x):
    return pltpu.with_memory_space_constraint(x, pltpu.HBM)


def pick(source, refs, store):
    for j, ref in enumerate(refs):

        @pl.when((source >> 1) == j)
        def _():
            store(ref, source & 1)


def pack_kernel(walkers_ref, counts_ref, slots_ref, top_ref, rest_ref, small_ref, sems):
    copies = [
        pltpu.make_async_copy(counts_ref, small_ref.at[0], sems.at[2]),
        pltpu.make_async_copy(slots_ref, small_ref.at[1], sems.at[3]),
        pltpu.make_async_copy(walkers_ref.at[:, 0, 0:NEL], top_ref.at[:, 0:NEL], sems.at[0]),
        pltpu.make_async_copy(walkers_ref.at[:, 0, NEL:M], rest_ref, sems.at[1]),
    ]
    for copy in copies:
        copy.start()
    copies[0].wait()
    copies[1].wait()
    row = lax.broadcasted_iota(jnp.int32, (16, NEL), 0)
    for i in range(2):
        values = jnp.where(row == 0, small_ref[0, i], small_ref[1, i])
        top_ref[i, NEL : NEL + 16] = values.astype(F32).astype(BF16)
    copies[2].wait()
    copies[3].wait()


def pack(walkers, counts, slots):
    return pl.pallas_call(
        pack_kernel,
        in_specs=[HBM, HBM, HBM],
        out_specs=[VM, VM],
        out_shape=[pltpu.VMEM((2, NEL + 16, NEL), BF16), pltpu.VMEM((2, M - NEL, NEL), BF16)],
        scratch_shapes=[pltpu.SMEM((2, 2), jnp.int32), pltpu.SemaphoreType.DMA((4,))],
        compiler_params=pltpu.CompilerParams(vmem_limit_bytes=4 * MIB),
        name="pack",
    )(held(walkers), held(counts[:, 0]), held(slots[:, 0]))


def own_kernel(local_ref, kept_ref, swapped_ref, out_ref, sem):
    @pl.when(local_ref[0] == 1)
    def _():
        copy = pltpu.make_async_copy(kept_ref, out_ref, sem)
        copy.start()
        copy.wait()

    @pl.when(local_ref[0] != 1)
    def _():
        copy = pltpu.make_async_copy(swapped_ref, out_ref, sem)
        copy.start()
        copy.wait()


def own_factor(local, kept, swapped):
    return pl.pallas_call(
        own_kernel,
        in_specs=[SM, HBM, HBM],
        out_specs=VM,
        out_shape=pltpu.VMEM(kept.shape, BF16),
        scratch_shapes=[pltpu.SemaphoreType.DMA],
        compiler_params=pltpu.CompilerParams(vmem_limit_bytes=2 * MIB),
        name="own",
    )(local, held(kept), held(swapped))


def stack_kernel(a_ref, b_ref, out_ref, sems):
    copies = [
        pltpu.make_async_copy(a_ref, out_ref.at[0], sems.at[0]),
        pltpu.make_async_copy(b_ref, out_ref.at[1], sems.at[1]),
    ]
    for copy in copies:
        copy.start()
    for copy in copies:
        copy.wait()


def stack(a, b):
    whole = pl.BlockSpec(memory_space=pl.ANY)
    return pl.pallas_call(
        stack_kernel,
        in_specs=[whole, whole],
        out_specs=VM,
        out_shape=pltpu.VMEM((2,) + a.shape, BF16),
        scratch_shapes=[pltpu.SemaphoreType.DMA((2,))],
        compiler_params=pltpu.CompilerParams(vmem_limit_bytes=4 * MIB),
        name="stack",
    )(a, b)


def find_sources(my, refs, src_ref):
    info = [[ref[i, NEL : NEL + 16, 0:128].astype(F32) for i in range(2)] for ref in refs]
    count = {(r, i): info[r][i][0:1] for r in range(4) for i in range(2)}
    position = {(r, i): (my ^ r) * 2 + i for r in range(4) for i in range(2)}
    upto = {}
    for here in count:
        total = count[here]
        for there in count:
            if there != here:
                total = total + jnp.where(position[there] < position[here], count[there], 0.0)
        upto[here] = total
    found = []
    for s in range(4):
        slot = info[s // 2][s % 2][1:2]
        chosen = jnp.zeros_like(slot)
        for r, i in count:
            inside = (upto[r, i] > slot) & (upto[r, i] - count[r, i] <= slot)
            chosen = chosen + jnp.where(inside, float(2 * r + i), 0.0)
        found.append(jnp.max(chosen).astype(jnp.int32))
        src_ref[s] = found[s]
    return found


def split(z_ref, value, high, low):
    upper = value.astype(BF16)
    z_ref[high] = upper
    z_ref[low] = (value - upper.astype(F32)).astype(BF16)


def square(x_ref, r_ref, z_ref, last=False):
    for s in range(4):
        split(z_ref, x_ref[s], 4 * s, 4 * s + 2)
        split(z_ref, r_ref[s], 4 * s + 1, 4 * s + 3)
    for s in range(4):
        rows = 3 if last else 4
        both = z_ref[4 * s : 4 * s + rows].reshape(rows * NEL, NEL)
        by_high = dot(both, z_ref[4 * s + 1])
        if last:
            by_low = dot(z_ref[4 * s], z_ref[4 * s + 3])
            r_ref[s] = by_high[NEL : 2 * NEL]
        else:
            by_low = dot(both[: 2 * NEL], z_ref[4 * s + 3])
            r_ref[s] = by_high[NEL : 2 * NEL] + (by_high[3 * NEL :] + by_low[NEL:])
        x_ref[s] = x_ref[s] + (by_high[:NEL] + (by_high[2 * NEL : 3 * NEL] + by_low[:NEL]))


def newton_kernel(my_ref, own_ref, core_ref, pair_ref, diag_ref, src_ref, new_ref, c_ref, x_ref, r_ref, z_ref):
    refs = (own_ref, core_ref, pair_ref, diag_ref)
    found = find_sources(my_ref[0], refs, src_ref)
    row = lax.broadcasted_iota(jnp.int32, (NEL, NEL), 0)
    col = lax.broadcasted_iota(jnp.int32, (NEL, NEL), 1)
    one = jnp.where(row == col, 1.0, 0.0).astype(F32)
    for s in range(4):

        def store(ref, i, s=s):
            if s < 2:
                new_ref[s, 0:NEL] = ref[i, 0:NEL]
            else:
                c_ref[s - 2] = ref[i, 0:NEL]

        pick(found[s], refs, store)
    for s in range(4):
        a = new_ref[s, 0:NEL] if s < 2 else c_ref[s - 2]
        residual = one - a.astype(F32)
        split(z_ref, residual, 4 * s + 1, 4 * s + 3)
        x_ref[s] = one + residual
    for s in range(4):
        high, low = z_ref[4 * s + 1], z_ref[4 * s + 3]
        r_ref[s] = dot(high, high) + (dot(high, low) + dot(low, high))

    def step(k, carry):
        square(x_ref, r_ref, z_ref)
        return carry

    lax.fori_loop(0, NEWTON - 5, step, 0)


def newton(my, own, core, pair, diag):
    return pl.pallas_call(
        newton_kernel,
        in_specs=[SM, VM, VM, VM, VM],
        out_specs=[SM] + [VM] * 4,
        out_shape=[
            jax.ShapeDtypeStruct((4,), jnp.int32),
            pltpu.VMEM((2, M, NEL), BF16),
            pltpu.VMEM((2, NEL, NEL), BF16),
            pltpu.VMEM((4, NEL, NEL), F32),
            pltpu.VMEM((4, NEL, NEL), F32),
        ],
        scratch_shapes=[pltpu.VMEM((16, NEL, NEL), BF16)],
        compiler_params=pltpu.CompilerParams(vmem_limit_bytes=16 * MIB),
        name="newton",
    )(my, own, core, pair, diag)


def inverse_kernel(x_in_ref, r_in_ref, new_ref, c_ref, inv_ref, green_ref, x_ref, r_ref, z_ref):
    x_ref[...] = x_in_ref[...]
    r_ref[...] = r_in_ref[...]

    def step(k, carry):
        square(x_ref, r_ref, z_ref)
        return carry

    lax.fori_loop(0, 2, step, 0)
    square(x_ref, r_ref, z_ref, last=True)
    for s in range(4):
        x = x_ref[s]
        inv = (x + dot(x.astype(BF16), r_ref[s].astype(BF16))).astype(BF16)
        inv_ref[s] = inv
        a = new_ref[s, 0:NEL] if s < 2 else c_ref[s - 2]
        green_ref[s, 0:NEL] = dot(a, inv).astype(BF16)


def inverse(x, r, new, c):
    return pl.pallas_call(
        inverse_kernel,
        in_specs=[VM] * 4,
        out_specs=[VM, VM],
        out_shape=[pltpu.VMEM((4, NEL, NEL), BF16), pltpu.VMEM((4, M, NEL), BF16)],
        scratch_shapes=[
            pltpu.VMEM((4, NEL, NEL), F32),
            pltpu.VMEM((4, NEL, NEL), F32),
            pltpu.VMEM((16, NEL, NEL), BF16),
        ],
        compiler_params=pltpu.CompilerParams(vmem_limit_bytes=16 * MIB),
        name="inverse",
    )(x, r, new, c)


def green_kernel(src_ref, own_ref, core_ref, pair_ref, diag_ref, inv_ref, *rest, at, rows):
    green_ref, new_ref, c_ref = rest[-3:]
    refs = (own_ref, core_ref, pair_ref, diag_ref)
    for s in range(4):

        def store(ref, i, s=s):
            if s < 2:
                new_ref[s, at : at + rows] = ref[i, 0:rows]
            else:
                c_ref[s - 2] = ref[i, 0:rows]

        pick(src_ref[s], refs, store)
    for s in range(4):
        c = new_ref[s, at : at + rows] if s < 2 else c_ref[s - 2]
        green_ref[s, at : at + rows] = dot(c, inv_ref[s]).astype(BF16)


def green_piece(src, own, core, pair, diag, inv, so_far, at, rows):
    carried = list(so_far)
    return pl.pallas_call(
        functools.partial(green_kernel, at=at, rows=rows),
        in_specs=[SM] + [VM] * (5 + len(carried)),
        out_specs=[VM, VM],
        out_shape=[pltpu.VMEM((4, M, NEL), BF16), pltpu.VMEM((2, M, NEL), BF16)],
        scratch_shapes=[pltpu.VMEM((2, rows, NEL), BF16)],
        input_output_aliases={6: 0, 7: 1},
        compiler_params=pltpu.CompilerParams(vmem_limit_bytes=16 * MIB),
    )(src, own, core, pair, diag, inv, *carried)


def load_blocks(refs):
    found = []
    for ref in refs:
        found += [ref[...]] if len(ref.shape) == 2 else [ref[i] for i in range(ref.shape[0])]
    return found


def count_blocks(arrays):
    return sum(1 if a.ndim == 2 else a.shape[0] for a in arrays)


def pair_products(blocks, green_ref, walkers, rot_ref):
    for l, f in enumerate(blocks):
        for i, w in enumerate(walkers):
            rot_ref[i * NEL : (i + 1) * NEL, l * NEL : (l + 1) * NEL] = dot(f, green_ref[w]).astype(BF16)
    return jnp.concatenate(blocks, axis=0)


def first_kernel(*refs, n):
    f_refs, green_ref, new_ref = refs[:n], refs[n], refs[n + 1]
    out_ref, combed_ref, rot_ref, sem = refs[n + 2 :]
    copy = pltpu.make_async_copy(new_ref, combed_ref.at[:, 0], sem)
    copy.start()
    stacked = pair_products(load_blocks(f_refs), green_ref, range(4), rot_ref)
    for m in range(0, M, NEL):
        out_ref[:, m : m + NEL] = dot(rot_ref[...], stacked[:, m : m + NEL])
    copy.wait()


def first_part(arrays, green, new):
    n, count = len(arrays), count_blocks(arrays)
    return pl.pallas_call(
        functools.partial(first_kernel, n=n),
        in_specs=[VM] * (n + 2),
        out_specs=[VM, pl.BlockSpec(memory_space=pl.ANY)],
        out_shape=[pltpu.VMEM((4 * NEL, M), F32), jax.ShapeDtypeStruct((2, 1, M, NEL), BF16)],
        scratch_shapes=[pltpu.VMEM((4 * NEL, count * NEL), BF16), pltpu.SemaphoreType.DMA],
        compiler_params=pltpu.CompilerParams(vmem_limit_bytes=24 * MIB),
        cost_estimate=pl.CostEstimate(
            flops=count * 16 * NEL * NEL * M, transcendentals=0, bytes_accessed=count * MIB // 2
        ),
    )(*arrays, green, new)


def main_kernel(*refs, n):
    f_refs, green_ref, acc_ref, out_ref, rot_ref = refs[:n], refs[n], refs[n + 1], refs[-2], refs[-1]
    stacked = pair_products(load_blocks(f_refs), green_ref, range(4), rot_ref)
    for m in range(0, M, NEL):
        out_ref[:, m : m + NEL] = acc_ref[:, m : m + NEL] + dot(rot_ref[...], stacked[:, m : m + NEL])


def main_part(arrays, green, running):
    n, count = len(arrays), count_blocks(arrays)
    return pl.pallas_call(
        functools.partial(main_kernel, n=n),
        in_specs=[VM] * (n + 2),
        out_specs=VM,
        out_shape=pltpu.VMEM((4 * NEL, M), F32),
        scratch_shapes=[pltpu.VMEM((4 * NEL, count * NEL), BF16)],
        input_output_aliases={n + 1: 0},
        compiler_params=pltpu.CompilerParams(vmem_limit_bytes=24 * MIB),
        cost_estimate=pl.CostEstimate(
            flops=count * 16 * NEL * NEL * M, transcendentals=0, bytes_accessed=count * MIB // 2
        ),
    )(*arrays, green, running)


def last_kernel(*refs, n, low):
    f_refs, green_ref, acc_ref, out_ref, rot_ref = refs[:n], refs[n], refs[n + 1], refs[-2], refs[-1]
    stacked = pair_products(load_blocks(f_refs), green_ref, (low, low + 1), rot_ref)
    for m in range(0, M, NEL):
        added = dot(rot_ref[...], stacked[:, m : m + NEL])
        total = acc_ref[low * NEL : (low + 2) * NEL, m : m + NEL] + added
        out_ref[:, m : m + NEL] = total.astype(out_ref.dtype)


def last_part(arrays, green, running, low, out_shape):
    n, count = len(arrays), count_blocks(arrays)
    return pl.pallas_call(
        functools.partial(last_kernel, n=n, low=low),
        in_specs=[VM] * (n + 2),
        out_specs=VM,
        out_shape=out_shape,
        scratch_shapes=[pltpu.VMEM((2 * NEL, count * NEL), BF16)],
        compiler_params=pltpu.CompilerParams(vmem_limit_bytes=24 * MIB),
        cost_estimate=pl.CostEstimate(
            flops=count * 8 * NEL * NEL * M, transcendentals=0, bytes_accessed=count * MIB // 2
        ),
    )(*arrays, green, running)


def combine_kernel(own_ref, other_ref, out_ref):
    out_ref[0, 0] = -(own_ref[...] + other_ref[...].astype(F32)).T


def combine(own, other):
    part = pl.BlockSpec((NEL, M), lambda w: (w, 0))
    return pl.pallas_call(
        combine_kernel,
        grid=(2,),
        in_specs=[part, part],
        out_specs=pl.BlockSpec((1, 1, M, NEL), lambda w: (w, 0, 0, 0)),
        out_shape=jax.ShapeDtypeStruct((2, 1, M, NEL), F32),
        compiler_params=pltpu.CompilerParams(vmem_limit_bytes=16 * MIB),
        name="combine",
    )(own, other)


def step(walkers, counts, slot_copy, factors):
    walk, chol = lax.axis_index("walk").astype(jnp.int32), lax.axis_index("chol").astype(jnp.int32)
    kept = factors.reshape(NEL, M)
    local = jnp.where((walk & 1) == (chol & 1), 1, 0).astype(jnp.int32).reshape(1)
    swapped = own_factor(local, kept, swap_factor(kept))
    top, rest = pack(walkers, counts, slot_copy)
    pair_top = to_pair(top)
    core_top = to_core(top)
    pair_rest = to_pair(rest)
    core_rest = to_core(rest)
    diag_top = to_core(pair_top)
    src, new, other_top, x, r = newton(walk.reshape(1), top, core_top, pair_top, diag_top)
    inv, green = inverse(x, r, new, other_top)

    f = {(0, 0): swapped}
    f[-1, 0] = first_along(kept, "a", 1)
    f[1, 0] = first_along(kept, "a", -1)
    f[0, -1] = along_b(swapped, 1)
    f[0, 1] = along_b(swapped, -1)
    f[2, 0] = moved(swapped, lambda xl, c, y, z, xh: (xl, c, *shifted(c, y, z, "a", 2), xh))
    sides = stack(f[-1, 0], f[1, 0])
    sides_below = along_b(sides, 1)
    sides_above = along_b(sides, -1)
    f[0, 2] = along_b(f[0, 1], -1)
    f[2, -1] = along_b(f[2, 0], 1)
    f[2, 1] = along_b(f[2, 0], -1)
    sides_far = along_b(sides_below, 1)
    f[2, 2] = along_b(f[2, 1], -1)

    diag_rest = to_core(pair_rest)
    green, new = green_piece(src, rest, core_rest, pair_rest, diag_rest, inv, (green, new), NEL, M - NEL)

    running, combed = first_part([f[0, 0], sides], green, new)
    running = main_part([f[2, 0], f[0, -1], f[0, 1]], green, running)
    running = main_part([sides_below, sides_above], green, running)
    running = main_part([f[2, -1], f[2, 1]], green, running)
    blocks = [f[0, 2], sides_far, f[2, 2]]
    half = (2 * NEL, M)
    other = to_core(last_part(blocks, green, running, 2, jax.ShapeDtypeStruct(half, BF16)))
    own = last_part(blocks, green, running, 0, pltpu.VMEM(half, F32))
    return combed, combine(own, other)


def solution(mesh):
    in_specs = (
        P("walk", "chol", None, None),
        P("walk", "chol"),
        P("walk", "chol"),
        P("chol", None, None),
    )
    out_specs = (P("walk", "chol", None, None), P("walk", "chol", None, None))
    return jax.shard_map(step, mesh=mesh, in_specs=in_specs, out_specs=out_specs, check_vma=False)
```

```python
import functools

import jax
import jax.numpy as jnp
from jax import lax
from jax.experimental import pallas as pl
from jax.experimental.pallas import tpu as pltpu
from jax.sharding import PartitionSpec as P

NEL = 256
M = 1024
NEWTON = 8
MIB = 1 << 20


BF16 = jnp.bfloat16
F32 = jnp.float32
VM = pl.BlockSpec(memory_space=pltpu.VMEM)
SM = pl.BlockSpec(memory_space=pltpu.SMEM)
HBM = pl.BlockSpec(memory_space=pltpu.HBM)


def dot(a, b):
    return jnp.dot(a, b, preferred_element_type=F32)


def line(x_lo, core, y, z, x_hi):
    return (x_lo * 2 + core) * 32 + (y * 4 + z) * 2 + x_hi


def moved(x, where):
    pairs = []
    for x_lo in range(2):
        for core in range(2):
            for y in range(4):
                for z in range(4):
                    for x_hi in range(2):
                        here = (x_lo, core, y, z, x_hi)
                        there = where(*here)
                        if there is not None:
                            pairs.append((line(*here), line(*there)))
    return lax.ppermute(x, ("walk", "chol"), pairs)


def to_core(x):
    return moved(x, lambda xl, c, y, z, xh: (xl, 1 - c, y, z, xh))


def to_pair(x):
    return moved(x, lambda xl, c, y, z, xh: (1 - xl, c, y, z, xh))


def swap_factor(x):
    def where(xl, c, y, z, xh):
        return None if c == xh else (1 - xl, 1 - c, y, z, 1 - xh)

    return moved(x, where)


def shifted(core, y, z, along, s):
    on_y = (core == 0) == (along == "a")
    return ((y + s) % 4, z) if on_y else (y, (z + s) % 4)


def first_along(x, along, s):
    def where(xl, c, y, z, xh):
        if c == xh:
            return (xl, c, *shifted(c, y, z, along, s), xh)
        return (1 - xl, 1 - c, *shifted(1 - c, y, z, along, s), 1 - xh)

    return moved(x, where)


def along_b(x, s):
    return moved(x, lambda xl, c, y, z, xh: (xl, c, *shifted(c, y, z, "b", s), xh))


def held(x):
    return pltpu.with_memory_space_constraint(x, pltpu.HBM)


def pick(source, refs, store):
    for j, ref in enumerate(refs):

        @pl.when((source >> 1) == j)
        def _():
            store(ref, source & 1)


def pack_kernel(walkers_ref, counts_ref, slots_ref, top_ref, rest_ref, small_ref, sems):
    copies = [
        pltpu.make_async_copy(counts_ref, small_ref.at[0], sems.at[2]),
        pltpu.make_async_copy(slots_ref, small_ref.at[1], sems.at[3]),
        pltpu.make_async_copy(walkers_ref.at[:, 0, 0:NEL], top_ref.at[:, 0:NEL], sems.at[0]),
        pltpu.make_async_copy(walkers_ref.at[:, 0, NEL:M], rest_ref, sems.at[1]),
    ]
    for copy in copies:
        copy.start()
    copies[0].wait()
    copies[1].wait()
    row = lax.broadcasted_iota(jnp.int32, (16, NEL), 0)
    for i in range(2):
        values = jnp.where(row == 0, small_ref[0, i], small_ref[1, i])
        top_ref[i, NEL : NEL + 16] = values.astype(F32).astype(BF16)
    copies[2].wait()
    copies[3].wait()


def pack(walkers, counts, slots):
    return pl.pallas_call(
        pack_kernel,
        in_specs=[HBM, HBM, HBM],
        out_specs=[VM, VM],
        out_shape=[pltpu.VMEM((2, NEL + 16, NEL), BF16), pltpu.VMEM((2, M - NEL, NEL), BF16)],
        scratch_shapes=[pltpu.SMEM((2, 2), jnp.int32), pltpu.SemaphoreType.DMA((4,))],
        compiler_params=pltpu.CompilerParams(vmem_limit_bytes=2 * MIB),
        name="pack",
    )(held(walkers), held(counts[:, 0]), held(slots[:, 0]))


def own_kernel(local_ref, kept_ref, swapped_ref, out_ref, sem):
    @pl.when(local_ref[0] == 1)
    def _():
        copy = pltpu.make_async_copy(kept_ref, out_ref, sem)
        copy.start()
        copy.wait()

    @pl.when(local_ref[0] != 1)
    def _():
        copy = pltpu.make_async_copy(swapped_ref, out_ref, sem)
        copy.start()
        copy.wait()


def own_factor(local, kept, swapped):
    return pl.pallas_call(
        own_kernel,
        in_specs=[SM, HBM, HBM],
        out_specs=VM,
        out_shape=pltpu.VMEM(kept.shape, BF16),
        scratch_shapes=[pltpu.SemaphoreType.DMA],
        compiler_params=pltpu.CompilerParams(vmem_limit_bytes=1 * MIB),
        name="own",
    )(local, held(kept), held(swapped))


def stack_kernel(a_ref, b_ref, out_ref, sems):
    copies = [
        pltpu.make_async_copy(a_ref, out_ref.at[0], sems.at[0]),
        pltpu.make_async_copy(b_ref, out_ref.at[1], sems.at[1]),
    ]
    for copy in copies:
        copy.start()
    for copy in copies:
        copy.wait()


def stack(a, b):
    whole = pl.BlockSpec(memory_space=pl.ANY)
    return pl.pallas_call(
        stack_kernel,
        in_specs=[whole, whole],
        out_specs=VM,
        out_shape=pltpu.VMEM((2,) + a.shape, BF16),
        scratch_shapes=[pltpu.SemaphoreType.DMA((2,))],
        compiler_params=pltpu.CompilerParams(vmem_limit_bytes=1 * MIB),
        name="stack",
    )(a, b)


def find_sources(my, refs, src_ref):
    info = [[ref[i, NEL : NEL + 16, 0:128].astype(F32) for i in range(2)] for ref in refs]
    count = {(r, i): info[r][i][0:1] for r in range(4) for i in range(2)}
    position = {(r, i): (my ^ r) * 2 + i for r in range(4) for i in range(2)}
    upto = {}
    for here in count:
        total = count[here]
        for there in count:
            if there != here:
                total = total + jnp.where(position[there] < position[here], count[there], 0.0)
        upto[here] = total
    found = []
    for s in range(4):
        slot = info[s // 2][s % 2][1:2]
        chosen = jnp.zeros_like(slot)
        for r, i in count:
            inside = (upto[r, i] > slot) & (upto[r, i] - count[r, i] <= slot)
            chosen = chosen + jnp.where(inside, float(2 * r + i), 0.0)
        found.append(jnp.max(chosen).astype(jnp.int32))
        src_ref[s] = found[s]
    return found


def split(z_ref, value, high, low):
    upper = value.astype(BF16)
    z_ref[high] = upper
    z_ref[low] = (value - upper.astype(F32)).astype(BF16)


def square(x_ref, r_ref, z_ref, last=False):
    for s in range(4):
        split(z_ref, x_ref[s], 4 * s, 4 * s + 2)
        split(z_ref, r_ref[s], 4 * s + 1, 4 * s + 3)
    for s in range(4):
        rows = 3 if last else 4
        both = z_ref[4 * s : 4 * s + rows].reshape(rows * NEL, NEL)
        by_high = dot(both, z_ref[4 * s + 1])
        if last:
            by_low = dot(z_ref[4 * s], z_ref[4 * s + 3])
            r_ref[s] = by_high[NEL : 2 * NEL]
        else:
            by_low = dot(both[: 2 * NEL], z_ref[4 * s + 3])
            r_ref[s] = by_high[NEL : 2 * NEL] + (by_high[3 * NEL :] + by_low[NEL:])
        x_ref[s] = x_ref[s] + (by_high[:NEL] + (by_high[2 * NEL : 3 * NEL] + by_low[:NEL]))


def newton_kernel(my_ref, own_ref, core_ref, pair_ref, diag_ref, src_ref, new_ref, c_ref, x_ref, r_ref, z_ref):
    refs = (own_ref, core_ref, pair_ref, diag_ref)
    found = find_sources(my_ref[0], refs, src_ref)
    row = lax.broadcasted_iota(jnp.int32, (NEL, NEL), 0)
    col = lax.broadcasted_iota(jnp.int32, (NEL, NEL), 1)
    one = jnp.where(row == col, 1.0, 0.0).astype(F32)
    for s in range(4):

        def store(ref, i, s=s):
            if s < 2:
                new_ref[s, 0:NEL] = ref[i, 0:NEL]
            else:
                c_ref[s - 2] = ref[i, 0:NEL]

        pick(found[s], refs, store)
    for s in range(4):
        a = new_ref[s, 0:NEL] if s < 2 else c_ref[s - 2]
        residual = one - a.astype(F32)
        split(z_ref, residual, 4 * s + 1, 4 * s + 3)
        x_ref[s] = one + residual
    for s in range(4):
        high, low = z_ref[4 * s + 1], z_ref[4 * s + 3]
        r_ref[s] = dot(high, high) + (dot(high, low) + dot(low, high))

    def step(k, carry):
        square(x_ref, r_ref, z_ref)
        return carry

    lax.fori_loop(0, NEWTON - 5, step, 0)


def newton(my, own, core, pair, diag):
    return pl.pallas_call(
        newton_kernel,
        in_specs=[SM, VM, VM, VM, VM],
        out_specs=[SM] + [VM] * 4,
        out_shape=[
            jax.ShapeDtypeStruct((4,), jnp.int32),
            pltpu.VMEM((2, M, NEL), BF16),
            pltpu.VMEM((2, NEL, NEL), BF16),
            pltpu.VMEM((4, NEL, NEL), F32),
            pltpu.VMEM((4, NEL, NEL), F32),
        ],
        scratch_shapes=[pltpu.VMEM((16, NEL, NEL), BF16)],
        compiler_params=pltpu.CompilerParams(vmem_limit_bytes=6 * MIB),
        name="newton",
    )(my, own, core, pair, diag)


def inverse_kernel(x_in_ref, r_in_ref, new_ref, c_ref, inv_ref, green_ref, x_ref, r_ref, z_ref):
    x_ref[...] = x_in_ref[...]
    r_ref[...] = r_in_ref[...]

    def step(k, carry):
        square(x_ref, r_ref, z_ref)
        return carry

    lax.fori_loop(0, 2, step, 0)
    square(x_ref, r_ref, z_ref, last=True)
    for s in range(4):
        x = x_ref[s]
        inv = (x + dot(x.astype(BF16), r_ref[s].astype(BF16))).astype(BF16)
        inv_ref[s] = inv
        a = new_ref[s, 0:NEL] if s < 2 else c_ref[s - 2]
        green_ref[s, 0:NEL] = dot(a, inv).astype(BF16)


def inverse(x, r, new, c):
    return pl.pallas_call(
        inverse_kernel,
        in_specs=[VM] * 4,
        out_specs=[VM, VM],
        out_shape=[pltpu.VMEM((4, NEL, NEL), BF16), pltpu.VMEM((4, M, NEL), BF16)],
        scratch_shapes=[
            pltpu.VMEM((4, NEL, NEL), F32),
            pltpu.VMEM((4, NEL, NEL), F32),
            pltpu.VMEM((16, NEL, NEL), BF16),
        ],
        compiler_params=pltpu.CompilerParams(vmem_limit_bytes=6 * MIB),
        name="inverse",
    )(x, r, new, c)


def green_kernel(src_ref, own_ref, core_ref, pair_ref, diag_ref, inv_ref, *rest, at, rows):
    green_ref, new_ref, c_ref = rest[-3:]
    refs = (own_ref, core_ref, pair_ref, diag_ref)
    for s in range(4):

        def store(ref, i, s=s):
            if s < 2:
                new_ref[s, at : at + rows] = ref[i, 0:rows]
            else:
                c_ref[s - 2] = ref[i, 0:rows]

        pick(src_ref[s], refs, store)
    for s in range(4):
        c = new_ref[s, at : at + rows] if s < 2 else c_ref[s - 2]
        green_ref[s, at : at + rows] = dot(c, inv_ref[s]).astype(BF16)


def green_piece(src, own, core, pair, diag, inv, so_far, at, rows):
    carried = list(so_far)
    return pl.pallas_call(
        functools.partial(green_kernel, at=at, rows=rows),
        in_specs=[SM] + [VM] * (5 + len(carried)),
        out_specs=[VM, VM],
        out_shape=[pltpu.VMEM((4, M, NEL), BF16), pltpu.VMEM((2, M, NEL), BF16)],
        scratch_shapes=[pltpu.VMEM((2, rows, NEL), BF16)],
        input_output_aliases={6: 0, 7: 1},
        compiler_params=pltpu.CompilerParams(vmem_limit_bytes=4 * MIB),
    )(src, own, core, pair, diag, inv, *carried)


def load_blocks(refs):
    found = []
    for ref in refs:
        found += [ref[...]] if len(ref.shape) == 2 else [ref[i] for i in range(ref.shape[0])]
    return found


def count_blocks(arrays):
    return sum(1 if a.ndim == 2 else a.shape[0] for a in arrays)


def pair_products(blocks, green_ref, walkers, rot_ref):
    for l, f in enumerate(blocks):
        for i, w in enumerate(walkers):
            rot_ref[i * NEL : (i + 1) * NEL, l * NEL : (l + 1) * NEL] = dot(f, green_ref[w]).astype(BF16)
    return jnp.concatenate(blocks, axis=0)


def first_kernel(*refs, n):
    f_refs, green_ref, new_ref = refs[:n], refs[n], refs[n + 1]
    out_ref, combed_ref, rot_ref, sem = refs[n + 2 :]
    copy = pltpu.make_async_copy(new_ref, combed_ref.at[:, 0], sem)
    copy.start()
    stacked = pair_products(load_blocks(f_refs), green_ref, range(4), rot_ref)
    for m in range(0, M, NEL):
        out_ref[:, m : m + NEL] = dot(rot_ref[...], stacked[:, m : m + NEL])
    copy.wait()


def first_part(arrays, green, new):
    n, count = len(arrays), count_blocks(arrays)
    return pl.pallas_call(
        functools.partial(first_kernel, n=n),
        in_specs=[VM] * (n + 2),
        out_specs=[VM, pl.BlockSpec(memory_space=pl.ANY)],
        out_shape=[pltpu.VMEM((4 * NEL, M), F32), jax.ShapeDtypeStruct((2, 1, M, NEL), BF16)],
        scratch_shapes=[pltpu.VMEM((4 * NEL, count * NEL), BF16), pltpu.SemaphoreType.DMA],
        compiler_params=pltpu.CompilerParams(vmem_limit_bytes=12 * MIB),
        cost_estimate=pl.CostEstimate(
            flops=count * 16 * NEL * NEL * M, transcendentals=0, bytes_accessed=count * MIB // 2
        ),
    )(*arrays, green, new)


def main_kernel(*refs, n):
    f_refs, green_ref, acc_ref, out_ref, rot_ref = refs[:n], refs[n], refs[n + 1], refs[-2], refs[-1]
    stacked = pair_products(load_blocks(f_refs), green_ref, range(4), rot_ref)
    for m in range(0, M, NEL):
        out_ref[:, m : m + NEL] = acc_ref[:, m : m + NEL] + dot(rot_ref[...], stacked[:, m : m + NEL])


def main_part(arrays, green, running):
    n, count = len(arrays), count_blocks(arrays)
    return pl.pallas_call(
        functools.partial(main_kernel, n=n),
        in_specs=[VM] * (n + 2),
        out_specs=VM,
        out_shape=pltpu.VMEM((4 * NEL, M), F32),
        scratch_shapes=[pltpu.VMEM((4 * NEL, count * NEL), BF16)],
        input_output_aliases={n + 1: 0},
        compiler_params=pltpu.CompilerParams(vmem_limit_bytes=12 * MIB),
        cost_estimate=pl.CostEstimate(
            flops=count * 16 * NEL * NEL * M, transcendentals=0, bytes_accessed=count * MIB // 2
        ),
    )(*arrays, green, running)


def last_kernel(*refs, n, low):
    f_refs, green_ref, acc_ref, out_ref, rot_ref = refs[:n], refs[n], refs[n + 1], refs[-2], refs[-1]
    stacked = pair_products(load_blocks(f_refs), green_ref, (low, low + 1), rot_ref)
    for m in range(0, M, NEL):
        added = dot(rot_ref[...], stacked[:, m : m + NEL])
        total = acc_ref[low * NEL : (low + 2) * NEL, m : m + NEL] + added
        out_ref[:, m : m + NEL] = total.astype(out_ref.dtype)


def last_part(arrays, green, running, low, out_shape):
    n, count = len(arrays), count_blocks(arrays)
    return pl.pallas_call(
        functools.partial(last_kernel, n=n, low=low),
        in_specs=[VM] * (n + 2),
        out_specs=VM,
        out_shape=out_shape,
        scratch_shapes=[pltpu.VMEM((2 * NEL, count * NEL), BF16)],
        compiler_params=pltpu.CompilerParams(vmem_limit_bytes=10 * MIB),
        cost_estimate=pl.CostEstimate(
            flops=count * 8 * NEL * NEL * M, transcendentals=0, bytes_accessed=count * MIB // 2
        ),
    )(*arrays, green, running)


def combine_kernel(own_ref, other_ref, out_ref):
    out_ref[0, 0] = -(own_ref[...] + other_ref[...].astype(F32)).T


def combine(own, other):
    part = pl.BlockSpec((NEL, M), lambda w: (w, 0))
    return pl.pallas_call(
        combine_kernel,
        grid=(2,),
        in_specs=[part, part],
        out_specs=pl.BlockSpec((1, 1, M, NEL), lambda w: (w, 0, 0, 0)),
        out_shape=jax.ShapeDtypeStruct((2, 1, M, NEL), F32),
        compiler_params=pltpu.CompilerParams(vmem_limit_bytes=8 * MIB),
        name="combine",
    )(own, other)


def step(walkers, counts, slot_copy, factors):
    walk, chol = lax.axis_index("walk").astype(jnp.int32), lax.axis_index("chol").astype(jnp.int32)
    kept = factors.reshape(NEL, M)
    local = jnp.where((walk & 1) == (chol & 1), 1, 0).astype(jnp.int32).reshape(1)
    swapped = own_factor(local, kept, swap_factor(kept))
    top, rest = pack(walkers, counts, slot_copy)
    pair_top = to_pair(top)
    core_top = to_core(top)
    pair_rest = to_pair(rest)
    core_rest = to_core(rest)
    diag_top = to_core(pair_top)
    src, new, other_top, x, r = newton(walk.reshape(1), top, core_top, pair_top, diag_top)
    inv, green = inverse(x, r, new, other_top)

    f = {(0, 0): swapped}
    f[-1, 0] = first_along(kept, "a", 1)
    f[1, 0] = first_along(kept, "a", -1)
    f[0, -1] = along_b(swapped, 1)
    f[0, 1] = along_b(swapped, -1)
    f[2, 0] = moved(swapped, lambda xl, c, y, z, xh: (xl, c, *shifted(c, y, z, "a", 2), xh))
    sides = stack(f[-1, 0], f[1, 0])
    sides_below = along_b(sides, 1)
    sides_above = along_b(sides, -1)
    f[0, 2] = along_b(f[0, 1], -1)
    f[2, -1] = along_b(f[2, 0], 1)
    f[2, 1] = along_b(f[2, 0], -1)
    sides_far = along_b(sides_below, 1)
    f[2, 2] = along_b(f[2, 1], -1)

    diag_rest = to_core(pair_rest)
    green, new = green_piece(src, rest, core_rest, pair_rest, diag_rest, inv, (green, new), NEL, M - NEL)

    running, combed = first_part([f[0, 0], sides], green, new)
    running = main_part([f[2, 0], f[0, -1], f[0, 1]], green, running)
    running = main_part([sides_below, sides_above], green, running)
    running = main_part([f[2, -1], f[2, 1], f[0, 2]], green, running)
    blocks = [sides_far, f[2, 2]]
    half = (2 * NEL, M)
    other = to_core(last_part(blocks, green, running, 2, jax.ShapeDtypeStruct(half, BF16)))
    own = last_part(blocks, green, running, 0, pltpu.VMEM(half, F32))
    return combed, combine(own, other)


def solution(mesh):
    in_specs = (
        P("walk", "chol", None, None),
        P("walk", "chol"),
        P("walk", "chol"),
        P("chol", None, None),
    )
    out_specs = (P("walk", "chol", None, None), P("walk", "chol", None, None))
    return jax.shard_map(step, mesh=mesh, in_specs=in_specs, out_specs=out_specs, check_vma=False)
```
